512 devices in a mesh: space: 32 (over z, x_lo), field: 16 (over x_hi, y, core).
Axes of the slice: x: 4 (x_hi: 2, x_lo: 2; x = x_hi * 2 + x_lo), y: 4, z: 16, core: 2. Of those that a mesh axis runs over, the one named last changes fastest.
Arguments:
- composition_vector: float32 [16, 32, 128, 16, 128], P('field', None, 'space'), may hold values from -6 to 6
- filtered_motion: float32 [3, 128, 16, 128], P(None, 'space', 'field'), may hold values from -1.8 to 1.8
- spreading_strength: float32 [128, 16, 128], P('space', 'field'), may hold values from 0.02 to 0.12
- blend_relax_multiplier: float32 [128, 16, 128], P('space', 'field'), may hold values from 0.2 to 0.9
- thermal_level: float32 [128, 16, 128], P('space', 'field'), may hold values from 0.5 to 2
- brownian_jumps: float32 [2, 16, 3], P(None, 'field'), may hold values from -2.5 to 2.5
- left_bilinear_weights: bfloat16 [206, 32], replicated, may hold values from -1 to 1
- right_bilinear_weights: bfloat16 [206, 32], replicated, may hold values from -1 to 1
- species_yield_weights: bfloat16 [32, 206], replicated, may hold values from -0.4375 to 0.4375
- arrhenius_prefactor: float32 [206], replicated, may hold values from 0.3 to 3
- ignition_energy_ratio: float32 [206], replicated, may hold values from 0.2 to 2
Outputs:
- result: float32 [16, 32, 128, 16, 128], P('field', None, 'space')
The draws below stay inside these ranges and needn't reach their ends.
All inputs are finite; a program needn't handle non-finite values.
Results may differ from the reference program's by a relative error of at most 0.00068.
Values sent between devices are 32-bit elements; how exact they have to be, the bound alone decides.
No kernel may reach another device: no remote copies, remote signals or barrier semaphores. Data moves between devices by JAX's collectives and lax.ppermute only.
A program may use at most 64 MiB of HBM per device.

```python
import math
import jax
import jax.numpy as jnp
from jax import lax

S = 32
R = 206
GRID_COUNT_Y = 16
GRID_COUNT_Z = 128
STEPS = 2
SUB = 5
FIELDS = 16
GRID_COUNT_X = 128


def shard_levels(own_key, extent, shards, smallest, high):
    factor_of = 1.0
    for position, blocks in shards:
        heights = jax.random.uniform(jax.random.fold_in(jax.random.fold_in(own_key, 6), position), (blocks,), jnp.float32, smallest / len(shards), high / len(shards))
        factor_of = factor_of * jnp.repeat(jnp.exp(heights), extent[position] // blocks).reshape((-1,) + (1,) * (len(extent) - 1 - position))
    return factor_of


def bell_draw(key, shape, spread, reach, cuts=(), dtype=jnp.bfloat16):
    array = spread * jax.random.normal(key, shape, jnp.float32)
    if cuts:
        array = array * shard_levels(key, shape, cuts, -0.22, 0.18)
    return jnp.clip(array, -reach, reach).astype(dtype)


def setup_inputs(seed: int = 0) -> dict:
    key_of = jax.random.split(jax.random.key(seed), 12)
    composition_vector = bell_draw(key_of[0], (FIELDS, S, GRID_COUNT_X, GRID_COUNT_Y, GRID_COUNT_Z), 1.0, 6.0, ((0, 16), (2, 32)), jnp.float32)
    filtered_motion = bell_draw(key_of[1], (3, GRID_COUNT_X, GRID_COUNT_Y, GRID_COUNT_Z), 0.3, 1.8, ((1, 32), (2, 16)), jnp.float32)
    spreading_strength = jnp.clip(0.02 + 0.09999999776482582 * jax.random.uniform(key_of[2], (GRID_COUNT_X, GRID_COUNT_Y, GRID_COUNT_Z), jnp.float32) ** shard_levels(key_of[2], (GRID_COUNT_X, GRID_COUNT_Y, GRID_COUNT_Z), ((0, 32), (1, 16)), -0.2, 0.2), 0.02, 0.12)
    blend_relax_multiplier = jnp.clip(0.2 + 0.7 * jax.random.uniform(key_of[3], (GRID_COUNT_X, GRID_COUNT_Y, GRID_COUNT_Z), jnp.float32) ** shard_levels(key_of[3], (GRID_COUNT_X, GRID_COUNT_Y, GRID_COUNT_Z), ((0, 32), (1, 16)), -0.2, 0.2), 0.2, 0.9)
    thermal_level = jnp.clip(0.5 + 1.5 * jax.random.uniform(key_of[4], (GRID_COUNT_X, GRID_COUNT_Y, GRID_COUNT_Z), jnp.float32) ** shard_levels(key_of[4], (GRID_COUNT_X, GRID_COUNT_Y, GRID_COUNT_Z), ((0, 32), (1, 16)), -0.2, 0.2), 0.5, 2.0)
    brownian_jumps = bell_draw(key_of[5], (STEPS, FIELDS, 3), 0.4, 2.5, ((1, 16),), jnp.float32)
    left_bilinear_weights = bell_draw(key_of[6], (R, S), S ** -0.5, 1.0)
    right_bilinear_weights = bell_draw(key_of[7], (R, S), S ** -0.5, 1.0)
    species_yield_weights = bell_draw(key_of[8], (S, R), R ** -0.5, 0.4375)
    arrhenius_prefactor = jnp.clip(jnp.exp(jax.random.uniform(key_of[9], (R,), jnp.float32, math.log(0.3), math.log(3.0))), 0.3, 3.0)
    ignition_energy_ratio = jnp.clip(jnp.exp(jax.random.uniform(key_of[10], (R,), jnp.float32, math.log(0.2), math.log(2.0))), 0.2, 2.0)
    return dict(composition_vector=composition_vector, filtered_motion=filtered_motion, spreading_strength=spreading_strength, blend_relax_multiplier=blend_relax_multiplier, thermal_level=thermal_level, brownian_jumps=brownian_jumps, left_bilinear_weights=left_bilinear_weights, right_bilinear_weights=right_bilinear_weights, species_yield_weights=species_yield_weights, arrhenius_prefactor=arrhenius_prefactor, ignition_energy_ratio=ignition_energy_ratio)


chem_step = 0.2

def transport(padded, current, mean, filtered_motion, spreading_strength, mixing, wiener):
    x_plus = padded[:, 2:]
    x_minus = padded[:, :-2]
    y_plus = jnp.roll(current, -1, 2)
    y_minus = jnp.roll(current, 1, 2)
    z_plus = jnp.roll(current, -1, 3)
    z_minus = jnp.roll(current, 1, 3)
    grad_x = 0.5 * (x_plus - x_minus)
    grad_y = 0.5 * (y_plus - y_minus)
    grad_z = 0.5 * (z_plus - z_minus)
    laplace = x_plus + x_minus + y_plus + y_minus + z_plus + z_minus - 6.0 * current
    advect = filtered_motion[0] * grad_x + filtered_motion[1] * grad_y + filtered_motion[2] * grad_z
    noise = jnp.sqrt(2.0 * spreading_strength) * (wiener[0] * grad_x + wiener[1] * grad_y + wiener[2] * grad_z)
    return current - advect + spreading_strength * laplace + noise - mixing * (current - mean)

def react(block, arrhenius, left_bilinear_weights, right_bilinear_weights, species_yield_weights):
    for substep in range(SUB):
        lowered = block.astype(jnp.bfloat16)
        forward = jnp.dot(left_bilinear_weights, lowered, preferred_element_type=jnp.float32)
        backward = jnp.dot(right_bilinear_weights, lowered, preferred_element_type=jnp.float32)
        saturation = 1.0 + forward * forward + backward * backward
        rates = (arrhenius * forward * backward / saturation).astype(jnp.bfloat16)
        block = block + chem_step * jnp.dot(species_yield_weights, rates, preferred_element_type=jnp.float32)
    return block

def kinetic_yield_term(carried_ensemble, thermal_level, arrhenius_prefactor, ignition_energy_ratio, left_bilinear_weights, right_bilinear_weights, species_yield_weights):
    species_count, planes, vertical_extent, streamwise_extent = carried_ensemble.shape

    def one_plane(plane_index, current):
        starting_ensemble = jnp.asarray(plane_index).astype(jnp.int32)
        block = lax.dynamic_slice_in_dim(current, starting_ensemble, 1, 1).reshape(species_count, vertical_extent * streamwise_extent)
        enthalpy_output = lax.dynamic_slice_in_dim(thermal_level, starting_ensemble, 1, 0).reshape(1, vertical_extent * streamwise_extent)
        arrhenius = arrhenius_prefactor[:, None] * jnp.exp(-ignition_energy_ratio[:, None] / enthalpy_output)
        reacted = react(block, arrhenius, left_bilinear_weights, right_bilinear_weights, species_yield_weights)
        reacted = reacted.reshape(species_count, 1, vertical_extent, streamwise_extent)
        return lax.dynamic_update_slice_in_dim(current, reacted, starting_ensemble, 1)
    return lax.fori_loop(0, planes, one_plane, carried_ensemble)

def reference(composition_vector, filtered_motion, spreading_strength, blend_relax_multiplier, thermal_level, brownian_jumps, left_bilinear_weights, right_bilinear_weights, species_yield_weights, arrhenius_prefactor, ignition_energy_ratio):
    for step in range(STEPS):
        mean = lax.optimization_barrier(jnp.sum(composition_vector, axis=0)) / FIELDS

        def one_field(pair):
            current, wiener = pair
            padded = jnp.concatenate([current[:, -1:], current, current[:, :1]], axis=1)
            carried_ensemble = transport(padded, current, mean, filtered_motion, spreading_strength, blend_relax_multiplier, wiener)
            return kinetic_yield_term(carried_ensemble, thermal_level, arrhenius_prefactor, ignition_energy_ratio, left_bilinear_weights, right_bilinear_weights, species_yield_weights)
        composition_vector = lax.map(one_field, (composition_vector, brownian_jumps[step]))
    return composition_vector
```

```python
import functools

import jax
import jax.numpy as jnp
from jax import lax
from jax.experimental import pallas as pl
from jax.experimental.pallas import tpu as pltpu
from jax.sharding import PartitionSpec as P

STEPS = 2
SUB = 5
CHEM_STEP = 0.2
F32, BF16 = jnp.float32, jnp.bfloat16
LANES = 128
VMEM = pl.BlockSpec(memory_space=pltpu.VMEM)


def lane_index(rows):
    return lax.broadcasted_iota(jnp.int32, (rows, LANES), 1)


def turn(x, shift):
    shift %= LANES
    return x if shift == 0 else pltpu.roll(x, shift, 1)


def swap_chunks(tiles, chunk):
    count = len(tiles)
    place = lane_index(tiles[0].shape[0]) // chunk
    step = 1
    while step < count:
        upper = (place // step) % 2 == 1
        fresh = list(tiles)
        for a in range(count):
            if (a // step) % 2 == 0:
                b = a + step
                fresh[a] = jnp.where(upper, turn(tiles[b], step * chunk), tiles[a])
                fresh[b] = jnp.where(upper, tiles[b], turn(tiles[a], -step * chunk))
        tiles = fresh
        step *= 2
    return tiles


def pack_kernel(cur, motion, spread, mix, therm, jumps, out):
    planes, rows, species, _ = cur.shape
    parts, chunk = rows, LANES // rows

    def one(i, _):
        x, g = i // (species // 8), i % (species // 8)
        at = pl.ds(pl.multiple_of(g * 8, 8), 8)
        tiles = swap_chunks([cur[x, y, at, :] for y in range(rows)], chunk)
        to = pl.ds(pl.multiple_of(x * species + g * 8, 8), 8)
        for j in range(parts):
            out[j, to, :] = tiles[j]
        return 0

    lax.fori_loop(0, planes * (species // 8), one, 0)
    lines = [motion[c, x] for c in range(3) for x in range(planes)]
    lines += [ref[x] for ref in (spread, mix, therm) for x in range(planes)]
    blocks = [jnp.concatenate(lines[8 * a : 8 * a + 8], axis=0) for a in range(3)]
    place = lane_index(8) // chunk
    line = lax.broadcasted_iota(jnp.int32, (8, LANES), 0)
    noise = jnp.zeros((8, LANES), F32)
    for r in range(3 * STEPS):
        noise = jnp.where(line == r, jumps[r // 3, 0, r % 3], noise)
    for j in range(parts):
        packed = jnp.where(place == 3, noise, turn(blocks[0], -chunk * j))
        for a in (1, 2):
            packed = jnp.where(place == a, turn(blocks[a], chunk * (a - j)), packed)
        out[j, planes * species :, :] = packed


def pack_z(read, low, high, fields, species, pairs):
    spot = lane_index(species) % 8
    for p, pair in enumerate(pairs):
        for g in range(fields // 4):
            first = last = None
            for k in range(8):
                tile = read(4 * g + k % 4, pair[k // 4])
                lo, hi = turn(tile, k), turn(tile, k - 7)
                first = lo if first is None else jnp.where(spot == k, lo, first)
                last = hi if last is None else jnp.where(spot == k, hi, last)
            low[p * (fields // 4) + g] = first
            high[p * (fields // 4) + g] = last


PAIRS = ((1, 2), (0, 3))


def open_kernel(planes, species, got, x_low, x_high, z_low, z_high, flow, wiener):
    fields = got.shape[0]
    chunk = LANES // fields
    read = lambda f, x: got[f, x * species : (x + 1) * species, :]
    for f in range(fields):
        x_low[f] = read(f, 0)
        x_high[f] = read(f, planes - 1)
    pack_z(read, z_low, z_high, fields, species, PAIRS)
    place = lane_index(8) // chunk
    for a in range(3):
        block = None
        for y in range(fields):
            piece = turn(got[y, planes * species :, :], chunk * (y - a))
            block = piece if block is None else jnp.where(place == y, piece, block)
        flow[8 * a : 8 * a + 8, :] = block
    for f in range(fields):
        noise = got[f, planes * species :, 3 * chunk : 3 * chunk + 1]
        wiener[f] = jnp.broadcast_to(noise, (8, LANES))


def step_kernel(step, halos, cur, before, after, z_after, z_before, flow, wiener, kinetics, left, right, gain, *rest):
    outs, (padded, means, arr, w, y) = rest[: 5 if halos else 1], rest[5 if halos else 1 :]
    out = outs[0]
    fields, species = before.shape[0], before.shape[1]
    planes = 4
    reactions = left.shape[0]
    ceil = w.shape[0] // 2
    w[...] = jnp.zeros_like(w)
    w[0:reactions, :] = left[...]
    w[ceil : ceil + reactions, :] = right[...]
    y[...] = jnp.zeros_like(y)
    y[:, 0:reactions] = gain[...]
    for f in range(fields):
        padded[0, f] = before[f]
        padded[planes + 1, f] = after[f]
        for x in range(planes):
            padded[x + 1, f] = cur[f, x * species : (x + 1) * species, :]
    spot = lane_index(species) % 8
    pre, energy = kinetics[:, 0:1], kinetics[:, 1:2]

    def plane(x, _):
        row = lambda c: flow[pl.ds(c * planes + x, 1), :]
        u = [row(0), row(1), row(2)]
        diffusion, mixing, heat = row(3), row(4), row(5)
        arr[...] = pre * jnp.exp(-energy / heat)
        total = padded[x + 1, 0]
        for f in range(1, fields):
            total = total + padded[x + 1, f]
        means[...] = (mixing * (1.0 / fields)) * total
        root = jnp.sqrt(2.0 * diffusion)
        inner = (x == 1) | (x == 2)
        pair = jnp.where(inner, 0, fields // 4)
        second = x >= 2
        centre = 1.0 - 6.0 * diffusion - mixing
        blocks = []
        for f in range(fields):
            here = padded[x + 1, f]
            sign = [0.5 * (root * wiener[f, 3 * step + d : 3 * step + d + 1, :] - u[d]) for d in range(3)]
            plus = [diffusion + s for s in sign]
            minus = [diffusion - s for s in sign]
            k = f % 4
            edge_after = z_after[pair + f // 4]
            edge_before = z_before[pair + f // 4]
            edge_after = jnp.where(second, turn(edge_after, 3 - k), turn(edge_after, 7 - k))
            edge_before = jnp.where(second, turn(edge_before, -4 - k), turn(edge_before, -k))
            z_plus = jnp.where(spot == 7, edge_after, turn(here, -1))
            z_minus = jnp.where(spot == 0, edge_before, turn(here, 1))
            moved = centre * here + means[...]
            moved = moved + plus[0] * padded[x + 2, f] + minus[0] * padded[x, f]
            moved = moved + plus[1] * turn(here, -8) + minus[1] * turn(here, 8)
            moved = moved + plus[2] * z_plus + minus[2] * z_minus
            blocks.append(moved)
        block = jnp.concatenate(blocks, axis=1)
        factor = jnp.concatenate([arr[...]] * fields, axis=1)
        for _ in range(SUB):
            low = block.astype(BF16)
            both = jnp.dot(w[...], low, preferred_element_type=F32)
            f, b = both[:ceil], both[ceil:]
            rates = (factor * f * b / (1.0 + f * f + b * b)).astype(BF16)
            block = block + CHEM_STEP * jnp.dot(y[...], rates, preferred_element_type=F32)
        to = pl.ds(pl.multiple_of(x * species, species), species)
        for f in range(fields):
            out[f, to, :] = block[:, f * LANES : (f + 1) * LANES]
        return 0

    lax.fori_loop(0, planes, plane, 0)
    if halos:
        x_low, x_high, z_low, z_high = outs[1:]
        read = lambda f, x: out[f, x * species : (x + 1) * species, :]
        for f in range(fields):
            x_low[f] = read(f, 0)
            x_high[f] = read(f, planes - 1)
        pack_z(read, z_low, z_high, fields, species, PAIRS)


def close_kernel(got, out):
    planes, rows, species, _ = out.shape
    chunk = LANES // rows

    def one(i, _):
        x, g = i // (species // 8), i % (species // 8)
        start = pl.ds(pl.multiple_of(x * species + g * 8, 8), 8)
        tiles = swap_chunks([got[j, start, :] for j in range(rows)], chunk)
        at = pl.ds(pl.multiple_of(g * 8, 8), 8)
        for y in range(rows):
            out[x, y, at, :] = tiles[y]
        return 0

    lax.fori_loop(0, planes * (species // 8), one, 0)


def shape(*dims):
    return jax.ShapeDtypeStruct(dims, F32)


def call(kernel, outs, ins, scratch=(), name=None, cost=None):
    return pl.pallas_call(
        kernel,
        out_shape=outs,
        in_specs=ins,
        out_specs=[VMEM] * len(outs) if isinstance(outs, (list, tuple)) else VMEM,
        scratch_shapes=list(scratch),
        name=name,
        cost_estimate=cost,
        compiler_params=pltpu.CompilerParams(vmem_limit_bytes=40 << 20),
    )


def neighbours(value_up, value_down, axis):
    count = lax.axis_size(axis)
    up = [(i, (i + 1) % count) for i in range(count)]
    down = [(j, i) for i, j in up]
    return lax.ppermute(value_up, axis, up), lax.ppermute(value_down, axis, down)


def body(comp, motion, spread, mix, therm, jumps, left, right, gain, prefactor, energy):
    fields = lax.axis_size("field")
    _, species, planes, rows, lanes = comp.shape
    reactions = left.shape[0]
    ceil = -(-reactions // 16) * 16
    cells = planes * species
    turned = comp[0].transpose(1, 2, 0, 3)
    sent = call(pack_kernel, shape(fields, cells + 8, lanes), [VMEM] * 5 + [pl.BlockSpec(memory_space=pltpu.SMEM)], name="pack")(
        turned, motion, spread, mix, therm, jumps
    )
    kinetics = jnp.pad(jnp.stack([prefactor, energy], 1), ((0, ceil - reactions), (0, 0)))
    cur = lax.all_to_all(sent, "field", 0, 0, tiled=True)
    edge = [shape(fields, species, lanes)] * 2 + [shape(fields // 2, species, lanes)] * 2
    *edges, flow, wiener = call(
        functools.partial(open_kernel, planes, species),
        edge + [shape(24, lanes), shape(fields, 8, lanes)],
        [VMEM],
        name="open",
    )(cur)
    flops = 2 * SUB * fields * planes * lanes * 3 * ceil * species
    for step in range(STEPS):
        before, after = neighbours(edges[1], edges[0], "space")
        z_before, z_after = neighbours(edges[3], edges[2], "field")
        last = step == STEPS - 1
        cur, *edges = call(
            functools.partial(step_kernel, step, not last),
            [shape(fields, cells, lanes)] + ([] if last else edge),
            [VMEM] * 11,
            scratch=[
                pltpu.VMEM((planes + 2, fields, species, lanes), F32),
                pltpu.VMEM((species, lanes), F32),
                pltpu.VMEM((ceil, lanes), F32),
                pltpu.VMEM((2 * ceil, species), BF16),
                pltpu.VMEM((species, ceil), BF16),
            ],
            name=f"step{step}",
            cost=pl.CostEstimate(flops=flops, bytes_accessed=4 << 20, transcendentals=0),
        )(cur, before, after, z_after, z_before, flow, wiener, kinetics, left, right, gain)
    got = lax.all_to_all(cur, "field", 0, 0, tiled=True)
    done = call(close_kernel, shape(planes, rows, species, lanes), [VMEM], name="close")(got)
    return done.transpose(2, 0, 1, 3)[None]


def solution(mesh):
    return jax.shard_map(
        body,
        mesh=mesh,
        in_specs=(
            P("field", None, "space", None, None),
            P(None, "space", "field", None),
            P("space", "field", None),
            P("space", "field", None),
            P("space", "field", None),
            P(None, "field", None),
            P(),
            P(),
            P(),
            P(),
            P(),
        ),
        out_specs=P("field", None, "space", None, None),
        check_vma=False,
    )
```

```python
import functools

import jax
import jax.numpy as jnp
from jax import lax
from jax.experimental import pallas as pl
from jax.experimental.pallas import tpu as pltpu
from jax.sharding import PartitionSpec as P

STEPS = 2
SUB = 5
CHEM_STEP = 0.2
F32, BF16 = jnp.float32, jnp.bfloat16
LANES = 128
VMEM = pl.BlockSpec(memory_space=pltpu.VMEM)
SMEM = pl.BlockSpec(memory_space=pltpu.SMEM)


def lane_index(rows):
    return lax.broadcasted_iota(jnp.int32, (rows, LANES), 1)


def turn(x, shift):
    shift %= LANES
    return x if shift == 0 else pltpu.roll(x, shift, 1)


def swap_chunks(tiles, chunk):
    count = len(tiles)
    place = lane_index(tiles[0].shape[0]) // chunk
    step = 1
    while step < count:
        upper = (place // step) % 2 == 1
        fresh = list(tiles)
        for a in range(count):
            if (a // step) % 2 == 0:
                b = a + step
                fresh[a] = jnp.where(upper, turn(tiles[b], step * chunk), tiles[a])
                fresh[b] = jnp.where(upper, tiles[b], turn(tiles[a], -step * chunk))
        tiles = fresh
        step *= 2
    return tiles


def pack_kernel(cur, motion, spread, mix, therm, jumps, out):
    planes, rows, species, _ = cur.shape
    parts, chunk = rows, LANES // rows
    groups = species // 8
    base = planes * species
    spot = lane_index(8) % chunk
    for half in range(planes * groups // chunk):
        before, after = [None] * parts, [None] * parts
        for k in range(chunk):
            x, g = divmod(half * chunk + k, groups)
            at = slice(8 * g, 8 * g + 8)
            tiles = swap_chunks([cur[x, y, at, :] for y in range(rows)], chunk)
            for j in range(parts):
                out[j, x * species + 8 * g : x * species + 8 * g + 8, :] = tiles[j]
                ends = turn(tiles[j - 1], k - chunk + 1), turn(tiles[(j + 1) % parts], k)
                before[j] = ends[0] if k == 0 else jnp.where(spot == k, ends[0], before[j])
                after[j] = ends[1] if k == 0 else jnp.where(spot == k, ends[1], after[j])
        for j in range(parts):
            out[j, base + 8 + 8 * half : base + 16 + 8 * half, :] = before[j]
            out[j, base + 24 + 8 * half : base + 32 + 8 * half, :] = after[j]
    lines = [motion[c, x] for c in range(3) for x in range(planes)]
    lines += [ref[x] for ref in (spread, mix, therm) for x in range(planes)]
    blocks = [jnp.concatenate(lines[8 * a : 8 * a + 8], axis=0) for a in range(3)]
    place = lane_index(8) // chunk
    line = lax.broadcasted_iota(jnp.int32, (8, LANES), 0)
    noise = jnp.zeros((8, LANES), F32)
    for r in range(3 * STEPS):
        noise = jnp.where(line == r, jumps[r // 3, 0, r % 3], noise)
    for j in range(parts):
        packed = jnp.where(place == 3, noise, turn(blocks[0], -chunk * j))
        for a in (1, 2):
            packed = jnp.where(place == a, turn(blocks[a], chunk * (a - j)), packed)
        out[j, base : base + 8, :] = packed


def open_kernel(species, got, x_low, x_high, flow, wiener):
    fields = got.shape[0]
    chunk = LANES // fields
    base = 4 * species
    for f in range(fields):
        x_low[f] = got[f, 0:species, :]
        x_high[f] = got[f, base - species : base, :]
    place = lane_index(8) // chunk
    for a in range(3):
        block = None
        for y in range(fields):
            piece = turn(got[y, base : base + 8, :], chunk * (y - a))
            block = piece if block is None else jnp.where(place == y, piece, block)
        flow[8 * a : 8 * a + 8, :] = block
    for f in range(fields):
        noise = got[f, base : base + 8, 3 * chunk : 3 * chunk + 1]
        wiener[f] = jnp.broadcast_to(noise, (8, LANES))


def pack_z(tiles, low, high):
    spot = lane_index(tiles[0].shape[1]) % 8
    for g in range(tiles[0].shape[0] // 4):
        first = last = None
        for k in range(8):
            tile = tiles[k // 4][4 * g + k % 4]
            lo, hi = turn(tile, k), turn(tile, k - 7)
            first = lo if k == 0 else jnp.where(spot == k, lo, first)
            last = hi if k == 0 else jnp.where(spot == k, hi, last)
        low[g] = first
        high[g] = last


def step_kernel(step, pair, *refs):
    flow, wiener, kinetics, left, right, gain, *refs = refs
    *refs, moved, arr, w, y = refs
    inner, last = pair == (1, 2), step == STEPS - 1
    fields = wiener.shape[0]
    species, reactions = gain.shape
    ceil = w.shape[0] // 2
    planes = 4
    base = planes * species
    spot = lane_index(species) % 8
    if step == 0:
        got, *refs = refs

        def tile(x, f):
            return got[f, x * species : (x + 1) * species, :]

        def edges(x, f):
            k = 4 * (x % 2)
            rows = base + 8 + 8 * (x // 2)
            behind, ahead = got[f, rows : rows + 8, :], got[f, rows + 16 : rows + 24, :]
            return (
                jnp.concatenate([turn(behind, -k - g) for g in range(4)], axis=0),
                jnp.concatenate([turn(ahead, 7 - k - g) for g in range(4)], axis=0),
            )

    else:
        *grid, z_before, z_after = refs[: planes + 2]
        refs = refs[planes + 2 :]

        def tile(x, f):
            return grid[x][f]

        def edges(x, f):
            k = 4 * pair.index(x) + f % 4
            return turn(z_before[f // 4], -k), turn(z_after[f // 4], 7 - k)

    if not inner:
        before, after, *refs = refs
    w[...] = jnp.zeros_like(w)
    w[0:reactions, :] = left[...]
    w[ceil : ceil + reactions, :] = right[...]
    y[...] = jnp.zeros_like(y)
    y[:, 0:reactions] = gain[...]
    for i, x in enumerate(pair):
        row = lambda c: flow[c * planes + x : c * planes + x + 1, :]
        u = [row(0), row(1), row(2)]
        diffusion, mixing = row(3), row(4)
        total = tile(x, 0)
        for f in range(1, fields):
            total = total + tile(x, f)
        mean = (mixing * (1.0 / fields)) * total
        root = jnp.sqrt(2.0 * diffusion)
        centre = 1.0 - 6.0 * diffusion - mixing
        for f in range(fields):
            here = tile(x, f)
            sign = [0.5 * (root * wiener[f, 3 * step + d : 3 * step + d + 1, :] - u[d]) for d in range(3)]
            plus = [diffusion + s for s in sign]
            minus = [diffusion - s for s in sign]
            behind, ahead = edges(x, f)
            x_plus = after[f] if x == planes - 1 else tile(x + 1, f)
            x_minus = before[f] if x == 0 else tile(x - 1, f)
            value = centre * here + mean
            value = value + plus[0] * x_plus + minus[0] * x_minus
            value = value + plus[1] * turn(here, -8) + minus[1] * turn(here, 8)
            value = value + plus[2] * jnp.where(spot == 7, ahead, turn(here, -1))
            value = value + minus[2] * jnp.where(spot == 0, behind, turn(here, 1))
            moved[i, :, f * LANES : (f + 1) * LANES] = value
    pre, energy = kinetics[:, 0:1], kinetics[:, 1:2]

    def chemistry(i, _):
        x = pair[0] + i * (pair[1] - pair[0])
        arr[...] = pre * jnp.exp(-energy / flow[pl.ds(5 * planes + x, 1), :])
        block = moved[i]
        factor = jnp.concatenate([arr[...]] * fields, axis=1)
        for _ in range(SUB):
            low = block.astype(BF16)
            both = jnp.dot(w[...], low, preferred_element_type=F32)
            f, b = both[:ceil], both[ceil:]
            rates = (factor * f * b / (1.0 + f * f + b * b)).astype(BF16)
            block = block + CHEM_STEP * jnp.dot(y[...], rates, preferred_element_type=F32)
        moved[i] = block
        return 0

    lax.fori_loop(0, 2, chemistry, 0)
    result = lambda i, f: moved[i, :, f * LANES : (f + 1) * LANES]
    if not last:
        for i in range(2):
            for f in range(fields):
                refs[i][f] = result(i, f)
        pack_z(refs[:2], *refs[2:])
    elif inner:
        for i in range(2):
            for f in range(fields):
                refs[0][f, i * species : (i + 1) * species, :] = result(i, f)
    else:
        middle, out = refs
        for f in range(fields):
            out[f, 0:species, :] = result(0, f)
            out[f, species : base - species, :] = middle[f]
            out[f, base - species : base, :] = result(1, f)


def close_kernel(got, out):
    planes, rows, species, _ = out.shape
    chunk = LANES // rows
    for x in range(planes):
        for g in range(species // 8):
            at = x * species + 8 * g
            tiles = swap_chunks([got[j, at : at + 8, :] for j in range(rows)], chunk)
            for y in range(rows):
                out[x, y, 8 * g : 8 * g + 8, :] = tiles[y]


def shape(*dims):
    return jax.ShapeDtypeStruct(dims, F32)


def call(kernel, outs, args, scratch=(), name=None, cost=None, scalars=()):
    many = isinstance(outs, (list, tuple))
    return pl.pallas_call(
        kernel,
        out_shape=outs,
        in_specs=[SMEM if i in scalars else VMEM for i in range(len(args))],
        out_specs=[VMEM] * len(outs) if many else VMEM,
        scratch_shapes=list(scratch),
        name=name,
        cost_estimate=cost,
        compiler_params=pltpu.CompilerParams(vmem_limit_bytes=40 << 20),
    )(*args)


def neighbours(value_up, value_down, axis):
    count = lax.axis_size(axis)
    up = [(i, (i + 1) % count) for i in range(count)]
    down = [(j, i) for i, j in up]
    return lax.ppermute(value_up, axis, up), lax.ppermute(value_down, axis, down)


def body(comp, motion, spread, mix, therm, jumps, left, right, gain, prefactor, energy):
    fields = lax.axis_size("field")
    _, species, planes, rows, lanes = comp.shape
    reactions = left.shape[0]
    ceil = -(-reactions // 16) * 16
    cells = planes * species
    turned = comp[0].transpose(1, 2, 0, 3)
    sent = call(
        pack_kernel,
        shape(fields, cells + 40, lanes),
        (turned, motion, spread, mix, therm, jumps),
        name="pack",
        scalars=(5,),
    )
    kinetics = jnp.pad(jnp.stack([prefactor, energy], 1), ((0, ceil - reactions), (0, 0)))
    got = lax.all_to_all(sent, "field", 0, 0, tiled=True)
    plane, edge = shape(fields, species, lanes), shape(fields // 4, species, lanes)
    x_low, x_high, flow, wiener = call(
        functools.partial(open_kernel, species),
        [plane, plane, shape(24, lanes), shape(fields, 8, lanes)],
        (got,),
        name="open",
    )
    flops = 2 * SUB * fields * 2 * lanes * 3 * ceil * species
    cost = pl.CostEstimate(flops=8 * flops, bytes_accessed=4 << 20, transcendentals=0)

    def advance(step, pair, outs, *args):
        return call(
            functools.partial(step_kernel, step, pair),
            outs,
            (flow, wiener, kinetics, left, right, gain, *args),
            scratch=[
                pltpu.VMEM((2, species, fields * lanes), F32),
                pltpu.VMEM((ceil, lanes), F32),
                pltpu.VMEM((2 * ceil, species), BF16),
                pltpu.VMEM((species, ceil), BF16),
            ],
            name=f"step{step}_{pair[0]}{pair[1]}",
            cost=cost,
        )

    middle, outer = (1, 2), (0, planes - 1)
    before, after = neighbours(x_high, x_low, "space")
    one, two, z_low, z_high = advance(0, middle, [plane, plane, edge, edge], got)
    z_middle = neighbours(z_high, z_low, "field")
    zero, three, z_low, z_high = advance(0, outer, [plane, plane, edge, edge], got, before, after)
    before, after = neighbours(three, zero, "space")
    z_outer = neighbours(z_high, z_low, "field")
    grid = (zero, one, two, three)
    part = advance(1, middle, shape(fields, cells // 2, lanes), *grid, *z_middle)
    done = advance(1, outer, shape(fields, cells, lanes), *grid, *z_outer, before, after, part)
    back = lax.all_to_all(done, "field", 0, 0, tiled=True)
    result = call(close_kernel, shape(planes, rows, species, lanes), (back,), name="close")
    return result.transpose(2, 0, 1, 3)[None]


def solution(mesh):
    return jax.shard_map(
        body,
        mesh=mesh,
        in_specs=(
            P("field", None, "space", None, None),
            P(None, "space", "field", None),
            P("space", "field", None),
            P("space", "field", None),
            P("space", "field", None),
            P(None, "field", None),
            P(),
            P(),
            P(),
            P(),
            P(),
        ),
        out_specs=P("field", None, "space", None, None),
        check_vma=False,
    )
```

```python
import functools

import jax
import jax.numpy as jnp
from jax import lax
from jax.experimental import pallas as pl
from jax.experimental.pallas import tpu as pltpu
from jax.sharding import PartitionSpec as P

STEPS = 2
SUB = 5
CHEM_STEP = 0.2
F32, BF16 = jnp.float32, jnp.bfloat16
LANES = 128
VMEM = pl.BlockSpec(memory_space=pltpu.VMEM)
SMEM = pl.BlockSpec(memory_space=pltpu.SMEM)


def lane_index(rows):
    return lax.broadcasted_iota(jnp.int32, (rows, LANES), 1)


def turn(x, shift):
    shift %= LANES
    return x if shift == 0 else pltpu.roll(x, shift, 1)


def bit(place, step):
    return (place // step) % 2 == 1


def gather_chunks(tiles, chunk):
    count = len(tiles)
    place = lane_index(tiles[0].shape[0]) // chunk
    tiles = [turn(tiles[-d], -chunk * d) for d in range(count)]
    step = 1
    while step < count:
        tiles = [jnp.where(bit(place, step), tiles[d - step], tiles[d]) for d in range(count)]
        step *= 2
    return tiles


def spread_chunks(tiles, chunk):
    count = len(tiles)
    place = lane_index(tiles[0].shape[0]) // chunk
    step = 1
    while step < count:
        tiles = [jnp.where(bit(place, step), tiles[(d + step) % count], tiles[d]) for d in range(count)]
        step *= 2
    return [turn(tiles[-y], -chunk * y) for y in range(count)]


def ring_order(count):
    half = count // 2
    return [k if k < half else half + 2 * ((count - 1 - k) // 2) + k % 2 for k in range(count)]


def pack_kernel(cur, motion, spread, mix, therm, jumps, out):
    planes, rows, species, _ = cur.shape
    parts, chunk = rows, LANES // rows
    order = ring_order(parts)
    groups = species // 8
    base = planes * species
    spot = lane_index(8) % chunk
    class_of = ((spot + 1) // 2) % 4
    for x in range(planes):
        ends = [None] * parts
        for g in range(groups):
            at = slice(8 * g, 8 * g + 8)
            tiles = gather_chunks([cur[x, y, at, :] for y in range(rows)], chunk)
            for k in range(parts):
                j = order[k]
                out[k, x * species + 8 * g : x * species + 8 * g + 8, :] = tiles[j]
                end = turn(jnp.where(spot == chunk - 1, tiles[j - 1], tiles[(j + 1) % parts]), -2 * g)
                ends[k] = end if g == 0 else jnp.where(class_of == 4 - g, end, ends[k])
        for k in range(parts):
            out[k, base + 8 + 8 * x : base + 16 + 8 * x, :] = ends[k]
    lines = [motion[c, x] for c in range(3) for x in range(planes)]
    lines += [ref[x] for ref in (spread, mix, therm) for x in range(planes)]
    blocks = [jnp.concatenate(lines[8 * a : 8 * a + 8], axis=0) for a in range(3)]
    place = lane_index(8) // chunk
    line = lax.broadcasted_iota(jnp.int32, (8, LANES), 0)
    noise = jnp.zeros((8, LANES), F32)
    for r in range(3 * STEPS):
        noise = jnp.where(line == r, jumps[r // 3, 0, r % 3], noise)
    for k in range(parts):
        j = order[k]
        packed = jnp.where(place == 3, noise, turn(blocks[0], -chunk * j))
        for a in (1, 2):
            packed = jnp.where(place == a, turn(blocks[a], chunk * (a - j)), packed)
        out[k, base : base + 8, :] = packed


def open_kernel(species, got, where, x_near, x_far, flow, wiener):
    fields = got.shape[0]
    chunk = LANES // fields
    base = 4 * species
    ring, odd = where[0], where[2]
    near = pl.multiple_of((base - species) * (1 - odd), 8)
    far = pl.multiple_of((base - species) * odd, 8)
    for f in range(fields):
        x_near[f] = got[f, pl.ds(near, species), :]
        x_far[f] = got[f, pl.ds(far, species), :]
    place = lane_index(8) // chunk
    for a in range(3):
        block = None
        for y in range(fields):
            piece = turn(got[y, base : base + 8, :], chunk * (y - a))
            block = piece if block is None else jnp.where(place == y, piece, block)
        flow[8 * a : 8 * a + 8, :] = pltpu.roll(block, chunk * ring, 1)
    for f in range(fields):
        noise = got[f, base : base + 8, 3 * chunk : 3 * chunk + 1]
        wiener[f] = jnp.broadcast_to(noise, (8, LANES))


def pack_z(tile, odd, near, far):
    groups, species, _ = near.shape
    spot = lane_index(species) % 8
    for g in range(groups):
        first = last = None
        for k in range(8):
            value = tile(k // 4, 4 * g + k % 4)
            lo, hi = turn(value, k), turn(value, -k)
            first = lo if k == 0 else jnp.where(spot == k, lo, first)
            last = hi if k == 0 else jnp.where(spot == 7 - k, hi, last)
        near[g] = jnp.where(odd, first, last)
        far[g] = jnp.where(odd, last, first)


def step_kernel(step, pair, *refs):
    where, flow, wiener, kinetics, left, right, gain, *refs = refs
    *refs, moved, arr, w, y = refs
    inner, last = pair == (1, 2), step == STEPS - 1
    fields = wiener.shape[0]
    species, reactions = gain.shape
    ceil = w.shape[0] // 2
    planes = 4
    base = planes * species
    spot = lane_index(species) % 8
    z_odd, x_odd = where[1] == 1, where[2] == 1
    if step == 0:
        got, *refs = refs

        def tile(x, f):
            return got[f, x * species : (x + 1) * species, :]

        def edges(x, f):
            rows = base + 8 + 8 * x
            packed = got[f, rows : rows + 8, :]
            value = jnp.concatenate([turn(packed, 2 * g) for g in range(4)], axis=0)
            return value, value

    else:
        *grid, z_near, z_far = refs[: planes + 2]
        refs = refs[planes + 2 :]

        def tile(x, f):
            return grid[x][f]

        def edges(x, f):
            k = 4 * pair.index(x) + f % 4
            near, far = z_near[f // 4], z_far[f // 4]
            return turn(jnp.where(z_odd, near, far), k), turn(jnp.where(z_odd, far, near), -k)

    if not inner:
        x_near, x_far, *refs = refs
    w[...] = jnp.zeros_like(w)
    w[0:reactions, :] = left[...]
    w[ceil : ceil + reactions, :] = right[...]
    y[...] = jnp.zeros_like(y)
    y[:, 0:reactions] = gain[...]
    for i, x in enumerate(pair):
        row = lambda c: flow[c * planes + x : c * planes + x + 1, :]
        u = [row(0), row(1), row(2)]
        diffusion, mixing = row(3), row(4)
        total = tile(x, 0)
        for f in range(1, fields):
            total = total + tile(x, f)
        mean = (mixing * (1.0 / fields)) * total
        root = jnp.sqrt(2.0 * diffusion)
        centre = 1.0 - 6.0 * diffusion - mixing
        for f in range(fields):
            here = tile(x, f)
            sign = [0.5 * (root * wiener[f, 3 * step + d : 3 * step + d + 1, :] - u[d]) for d in range(3)]
            plus = [diffusion + s for s in sign]
            minus = [diffusion - s for s in sign]
            behind, ahead = edges(x, f)
            if x == planes - 1:
                x_plus = jnp.where(x_odd, x_far[f], x_near[f])
            else:
                x_plus = tile(x + 1, f)
            if x == 0:
                x_minus = jnp.where(x_odd, x_near[f], x_far[f])
            else:
                x_minus = tile(x - 1, f)
            value = centre * here + mean
            value = value + plus[0] * x_plus + minus[0] * x_minus
            value = value + plus[1] * turn(here, -8) + minus[1] * turn(here, 8)
            value = value + plus[2] * turn(jnp.where(spot == 0, ahead, here), -1)
            value = value + minus[2] * turn(jnp.where(spot == 7, behind, here), 1)
            moved[i, :, f * LANES : (f + 1) * LANES] = value
    pre, energy = kinetics[:, 0:1], kinetics[:, 1:2]

    def chemistry(i, _):
        x = pair[0] + i * (pair[1] - pair[0])
        arr[...] = pre * jnp.exp(-energy / flow[pl.ds(5 * planes + x, 1), :])
        block = moved[i]
        factor = jnp.concatenate([arr[...]] * fields, axis=1)
        for _ in range(SUB):
            low = block.astype(BF16)
            both = jnp.dot(w[...], low, preferred_element_type=F32)
            f, b = both[:ceil], both[ceil:]
            rates = (factor * f * b / (1.0 + f * f + b * b)).astype(BF16)
            block = block + CHEM_STEP * jnp.dot(y[...], rates, preferred_element_type=F32)
        moved[i] = block
        return 0

    lax.fori_loop(0, 2, chemistry, 0)
    result = lambda i, f: moved[i, :, f * LANES : (f + 1) * LANES]
    if not last:
        for i in range(2):
            for f in range(fields):
                refs[i][f] = result(i, f)
        pack_z(result, z_odd, *refs[2:4])
        if not inner:
            for f in range(fields):
                refs[4][f] = result(1 - where[2], f)
                refs[5][f] = result(where[2], f)
    elif inner:
        for i in range(2):
            for f in range(fields):
                refs[0][f, i * species : (i + 1) * species, :] = result(i, f)
    else:
        middle, out = refs
        for f in range(fields):
            out[f, 0:species, :] = result(0, f)
            out[f, species : base - species, :] = middle[f]
            out[f, base - species : base, :] = result(1, f)


def close_kernel(got, out):
    planes, rows, species, _ = out.shape
    chunk = LANES // rows
    order = ring_order(rows)
    for x in range(planes):
        for g in range(species // 8):
            at = x * species + 8 * g
            tiles = [got[order.index(j), at : at + 8, :] for j in range(rows)]
            tiles = spread_chunks(tiles, chunk)
            for y in range(rows):
                out[x, y, 8 * g : 8 * g + 8, :] = tiles[y]


def shape(*dims):
    return jax.ShapeDtypeStruct(dims, F32)


def call(kernel, outs, args, scratch=(), name=None, cost=None, scalars=()):
    many = isinstance(outs, (list, tuple))
    return pl.pallas_call(
        kernel,
        out_shape=outs,
        in_specs=[SMEM if i in scalars else VMEM for i in range(len(args))],
        out_specs=[VMEM] * len(outs) if many else VMEM,
        scratch_shapes=list(scratch),
        name=name,
        cost_estimate=cost,
        compiler_params=pltpu.CompilerParams(vmem_limit_bytes=40 << 20),
    )(*args)


def swaps(near, far, axis, order):
    count = len(order)
    pairs = lambda first: [
        (order.index((q + first) % count), order.index((p + first) % count))
        for i in range(0, count, 2)
        for p, q in ((i, i + 1), (i + 1, i))
    ]
    return lax.ppermute(near, axis, pairs(0)), lax.ppermute(far, axis, pairs(1))


def body(comp, motion, spread, mix, therm, jumps, left, right, gain, prefactor, energy):
    fields = lax.axis_size("field")
    _, species, planes, rows, lanes = comp.shape
    reactions = left.shape[0]
    ceil = -(-reactions // 16) * 16
    cells = planes * species
    turned = comp[0].transpose(1, 2, 0, 3)
    sent = call(
        pack_kernel,
        shape(fields, cells + 40, lanes),
        (turned, motion, spread, mix, therm, jumps),
        name="pack",
        scalars=(5,),
    )
    order, line = ring_order(fields), list(range(lax.axis_size("space")))
    ring = jnp.asarray(order, jnp.int32)[lax.axis_index("field")]
    where = jnp.stack([ring, ring % 2, lax.axis_index("space") % 2]).astype(jnp.int32)
    kinetics = jnp.pad(jnp.stack([prefactor, energy], 1), ((0, ceil - reactions), (0, 0)))
    got = lax.all_to_all(sent, "field", 0, 0, tiled=True)
    plane, edge = shape(fields, species, lanes), shape(fields // 4, species, lanes)
    x_near, x_far, flow, wiener = call(
        functools.partial(open_kernel, species),
        [plane, plane, shape(24, lanes), shape(fields, 8, lanes)],
        (got, where),
        name="open",
        scalars=(1,),
    )
    flops = 2 * SUB * fields * 2 * lanes * 3 * ceil * species
    cost = pl.CostEstimate(flops=8 * flops, bytes_accessed=4 << 20, transcendentals=0)

    def advance(step, pair, outs, *args):
        return call(
            functools.partial(step_kernel, step, pair),
            outs,
            (where, flow, wiener, kinetics, left, right, gain, *args),
            scalars=(0,),
            scratch=[
                pltpu.VMEM((2, species, fields * lanes), F32),
                pltpu.VMEM((ceil, lanes), F32),
                pltpu.VMEM((2 * ceil, species), BF16),
                pltpu.VMEM((species, ceil), BF16),
            ],
            name=f"step{step}_{pair[0]}{pair[1]}",
            cost=cost,
        )

    middle, outer = (1, 2), (0, planes - 1)
    x_halo = swaps(x_near, x_far, "space", line)
    one, two, *z_ends = advance(0, middle, [plane, plane, edge, edge], got)
    z_middle = swaps(*z_ends, "field", order)
    zero, three, *ends = advance(0, outer, [plane, plane, edge, edge, plane, plane], got, *x_halo)
    z_outer = swaps(*ends[:2], "field", order)
    x_halo = swaps(*ends[2:], "space", line)
    grid = (zero, one, two, three)
    part = advance(1, middle, shape(fields, cells // 2, lanes), *grid, *z_middle)
    done = advance(1, outer, shape(fields, cells, lanes), *grid, *z_outer, *x_halo, part)
    back = lax.all_to_all(done, "field", 0, 0, tiled=True)
    result = call(close_kernel, shape(planes, rows, species, lanes), (back,), name="close")
    return result.transpose(2, 0, 1, 3)[None]


def solution(mesh):
    return jax.shard_map(
        body,
        mesh=mesh,
        in_specs=(
            P("field", None, "space", None, None),
            P(None, "space", "field", None),
            P("space", "field", None),
            P("space", "field", None),
            P("space", "field", None),
            P(None, "field", None),
            P(),
            P(),
            P(),
            P(),
            P(),
        ),
        out_specs=P("field", None, "space", None, None),
        check_vma=False,
    )
```

```python
import functools

import jax
import jax.numpy as jnp
from jax import lax
from jax.experimental import pallas as pl
from jax.experimental.pallas import tpu as pltpu
from jax.sharding import PartitionSpec as P

STEPS = 2
SUB = 5
CHEM_STEP = 0.2
F32, BF16 = jnp.float32, jnp.bfloat16
LANES = 128
VMEM = pl.BlockSpec(memory_space=pltpu.VMEM)
SMEM = pl.BlockSpec(memory_space=pltpu.SMEM)


def lane_index(rows):
    return lax.broadcasted_iota(jnp.int32, (rows, LANES), 1)


def turn(x, shift):
    shift %= LANES
    return x if shift == 0 else pltpu.roll(x, shift, 1)


def bit(place, step):
    return (place // step) % 2 == 1


def gather_chunks(tiles, chunk):
    count = len(tiles)
    place = lane_index(tiles[0].shape[0]) // chunk
    tiles = [turn(tiles[-d], -chunk * d) for d in range(count)]
    step = 1
    while step < count:
        tiles = [jnp.where(bit(place, step), tiles[d - step], tiles[d]) for d in range(count)]
        step *= 2
    return tiles


def spread_chunks(tiles, chunk):
    count = len(tiles)
    place = lane_index(tiles[0].shape[0]) // chunk
    step = 1
    while step < count:
        tiles = [jnp.where(bit(place, step), tiles[(d + step) % count], tiles[d]) for d in range(count)]
        step *= 2
    return [turn(tiles[-y], -chunk * y) for y in range(count)]


def ring_order(count):
    half = count // 2
    return [k if k < half else half + 2 * ((count - 1 - k) // 2) + k % 2 for k in range(count)]


def pack_kernel(cur, motion, spread, mix, therm, jumps, out):
    planes, rows, species, _ = cur.shape
    parts, chunk = rows, LANES // rows
    order = ring_order(parts)
    groups = species // 8
    base = planes * species
    spot = lane_index(8) % chunk
    class_of = ((spot + 1) // 2) % 4
    for x in range(planes):
        ends = [None] * parts
        for g in range(groups):
            at = slice(8 * g, 8 * g + 8)
            tiles = gather_chunks([cur[x, y, at, :] for y in range(rows)], chunk)
            for k in range(parts):
                j = order[k]
                out[k, x * species + 8 * g : x * species + 8 * g + 8, :] = tiles[j]
                end = turn(jnp.where(spot == chunk - 1, tiles[j - 1], tiles[(j + 1) % parts]), -2 * g)
                ends[k] = end if g == 0 else jnp.where(class_of == 4 - g, end, ends[k])
        for k in range(parts):
            out[k, base + 8 + 8 * x : base + 16 + 8 * x, :] = ends[k]
    lines = [motion[c, x] for c in range(3) for x in range(planes)]
    lines += [ref[x] for ref in (spread, mix, therm) for x in range(planes)]
    blocks = [jnp.concatenate(lines[8 * a : 8 * a + 8], axis=0) for a in range(3)]
    place = lane_index(8) // chunk
    line = lax.broadcasted_iota(jnp.int32, (8, LANES), 0)
    noise = jnp.zeros((8, LANES), F32)
    for r in range(3 * STEPS):
        noise = jnp.where(line == r, jumps[r // 3, 0, r % 3], noise)
    for k in range(parts):
        j = order[k]
        packed = jnp.where(place == 3, noise, turn(blocks[0], -chunk * j))
        for a in (1, 2):
            packed = jnp.where(place == a, turn(blocks[a], chunk * (a - j)), packed)
        out[k, base : base + 8, :] = packed


def open_kernel(species, got, where, x_near, x_far, flow, wiener):
    fields = got.shape[0]
    chunk = LANES // fields
    base = 4 * species
    ring, odd = where[0:8, :], where[16:17, :] == 1
    for f in range(fields):
        first, last = got[f, 0:species, :], got[f, base - species : base, :]
        x_near[f] = jnp.where(odd, first, last)
        x_far[f] = jnp.where(odd, last, first)
    place = lane_index(8) // chunk
    for a in range(3):
        block = None
        for y in range(fields):
            piece = turn(got[y, base : base + 8, :], chunk * (y - a))
            block = piece if block is None else jnp.where(place == y, piece, block)
        step = 1
        while step < fields:
            block = jnp.where(bit(ring, step), turn(block, chunk * step), block)
            step *= 2
        flow[8 * a : 8 * a + 8, :] = block
    for f in range(fields):
        noise = got[f, base : base + 8, 3 * chunk : 3 * chunk + 1]
        wiener[f] = jnp.broadcast_to(noise, (8, LANES))


def pack_z(tile, odd, near, far):
    groups, species, _ = near.shape
    spot = lane_index(species) % 8
    for g in range(groups):
        first = last = None
        for k in range(8):
            value = tile(k // 4, 4 * g + k % 4)
            lo, hi = turn(value, k), turn(value, -k)
            first = lo if k == 0 else jnp.where(spot == k, lo, first)
            last = hi if k == 0 else jnp.where(spot == 7 - k, hi, last)
        near[g] = jnp.where(odd, first, last)
        far[g] = jnp.where(odd, last, first)


def step_kernel(step, pair, *refs):
    where, flow, wiener, kinetics, left, right, gain, *refs = refs
    *refs, moved, arr, w, y = refs
    inner, last = pair == (1, 2), step == STEPS - 1
    fields = wiener.shape[0]
    species, reactions = gain.shape
    ceil = w.shape[0] // 2
    planes = 4
    base = planes * species
    spot = lane_index(species) % 8
    z_odd, x_odd = where[8:9, :] == 1, where[16:17, :] == 1
    if step == 0:
        got, *refs = refs

        def tile(x, f):
            return got[f, x * species : (x + 1) * species, :]

        def edges(x, f):
            rows = base + 8 + 8 * x
            packed = got[f, rows : rows + 8, :]
            value = jnp.concatenate([turn(packed, 2 * g) for g in range(4)], axis=0)
            return value, value

    else:
        *grid, z_near, z_far = refs[: planes + 2]
        refs = refs[planes + 2 :]

        def tile(x, f):
            return grid[x][f]

        def edges(x, f):
            k = 4 * pair.index(x) + f % 4
            near, far = z_near[f // 4], z_far[f // 4]
            return turn(jnp.where(z_odd, near, far), k), turn(jnp.where(z_odd, far, near), -k)

    if not inner:
        x_near, x_far, *refs = refs
    w[...] = jnp.zeros_like(w)
    for c in range(0, reactions, 16):
        end = min(c + 16, reactions)
        w[2 * c : 2 * c + end - c, :] = left[c:end, :]
        w[2 * c + 16 : 2 * c + 16 + end - c, :] = right[c:end, :]
    y[...] = jnp.zeros_like(y)
    y[:, 0:reactions] = gain[...]
    for i, x in enumerate(pair):
        row = lambda c: flow[c * planes + x : c * planes + x + 1, :]
        u = [row(0), row(1), row(2)]
        diffusion, mixing = row(3), row(4)
        total = tile(x, 0)
        for f in range(1, fields):
            total = total + tile(x, f)
        mean = (mixing * (1.0 / fields)) * total
        root = jnp.sqrt(2.0 * diffusion)
        centre = 1.0 - 6.0 * diffusion - mixing
        for f in range(fields):
            here = tile(x, f)
            sign = [0.5 * (root * wiener[f, 3 * step + d : 3 * step + d + 1, :] - u[d]) for d in range(3)]
            plus = [diffusion + s for s in sign]
            minus = [diffusion - s for s in sign]
            behind, ahead = edges(x, f)
            if x == planes - 1:
                x_plus = jnp.where(x_odd, x_far[f], x_near[f])
            else:
                x_plus = tile(x + 1, f)
            if x == 0:
                x_minus = jnp.where(x_odd, x_near[f], x_far[f])
            else:
                x_minus = tile(x - 1, f)
            value = centre * here + mean
            value = value + plus[0] * x_plus + minus[0] * x_minus
            value = value + plus[1] * turn(here, -8) + minus[1] * turn(here, 8)
            value = value + plus[2] * turn(jnp.where(spot == 0, ahead, here), -1)
            value = value + minus[2] * turn(jnp.where(spot == 7, behind, here), 1)
            moved[i, :, f * LANES : (f + 1) * LANES] = value
    pre, energy = kinetics[:, 0:1], kinetics[:, 1:2]
    count = 4
    wide = fields * LANES // count

    def chemistry(i, _):
        x = pair[0] + i * (pair[1] - pair[0])
        arr[...] = pre * jnp.exp(-energy / flow[pl.ds(5 * planes + x, 1), :])
        factor = jnp.concatenate([arr[...]] * (wide // LANES), axis=1)
        blocks = [moved[i, :, j * wide : (j + 1) * wide] for j in range(count)]

        def factors(j):
            low = blocks[j].astype(BF16)
            return [
                jnp.dot(w[2 * c : 2 * c + 32, :], low, preferred_element_type=F32)
                for c in range(0, ceil, 16)
            ]

        ahead = factors(0)
        for n in range(SUB * count):
            now, j = ahead, n % count
            if n + 1 < SUB * count:
                ahead = factors((n + 1) % count)
            rates = []
            for c, both in enumerate(now):
                f, b = both[:16], both[16:]
                scaled = factor[16 * c : 16 * c + 16] * f * b
                rates.append((scaled / (1.0 + f * f + b * b)).astype(BF16))
            rates = jnp.concatenate(rates, axis=0)
            blocks[j] = blocks[j] + CHEM_STEP * jnp.dot(y[...], rates, preferred_element_type=F32)
        for j in range(count):
            moved[i, :, j * wide : (j + 1) * wide] = blocks[j]
        return 0

    lax.fori_loop(0, 2, chemistry, 0)
    result = lambda i, f: moved[i, :, f * LANES : (f + 1) * LANES]
    if not last:
        for i in range(2):
            for f in range(fields):
                refs[i][f] = result(i, f)
        pack_z(result, z_odd, *refs[2:4])
        if not inner:
            for f in range(fields):
                refs[4][f] = jnp.where(x_odd, result(0, f), result(1, f))
                refs[5][f] = jnp.where(x_odd, result(1, f), result(0, f))
    elif inner:
        for i in range(2):
            for f in range(fields):
                refs[0][f, i * species : (i + 1) * species, :] = result(i, f)
    else:
        middle, out = refs
        for f in range(fields):
            out[f, 0:species, :] = result(0, f)
            out[f, species : base - species, :] = middle[f]
            out[f, base - species : base, :] = result(1, f)


def close_kernel(got, out):
    planes, rows, species, _ = out.shape
    chunk = LANES // rows
    order = ring_order(rows)
    for x in range(planes):
        for g in range(species // 8):
            at = x * species + 8 * g
            tiles = [got[order.index(j), at : at + 8, :] for j in range(rows)]
            tiles = spread_chunks(tiles, chunk)
            for y in range(rows):
                out[x, y, 8 * g : 8 * g + 8, :] = tiles[y]


def shape(*dims):
    return jax.ShapeDtypeStruct(dims, F32)


def call(kernel, outs, args, scratch=(), name=None, cost=None, scalars=()):
    many = isinstance(outs, (list, tuple))
    return pl.pallas_call(
        kernel,
        out_shape=outs,
        in_specs=[SMEM if i in scalars else VMEM for i in range(len(args))],
        out_specs=[VMEM] * len(outs) if many else VMEM,
        scratch_shapes=list(scratch),
        name=name,
        cost_estimate=cost,
        compiler_params=pltpu.CompilerParams(vmem_limit_bytes=40 << 20),
    )(*args)


def swaps(near, far, axis, order):
    count = len(order)
    pairs = lambda first: [
        (order.index((q + first) % count), order.index((p + first) % count))
        for i in range(0, count, 2)
        for p, q in ((i, i + 1), (i + 1, i))
    ]
    return lax.ppermute(near, axis, pairs(0)), lax.ppermute(far, axis, pairs(1))


def body(comp, motion, spread, mix, therm, jumps, left, right, gain, prefactor, energy):
    fields = lax.axis_size("field")
    _, species, planes, rows, lanes = comp.shape
    reactions = left.shape[0]
    ceil = -(-reactions // 16) * 16
    cells = planes * species
    turned = comp[0].transpose(1, 2, 0, 3)
    sent = call(
        pack_kernel,
        shape(fields, cells + 40, lanes),
        (turned, motion, spread, mix, therm, jumps),
        name="pack",
        scalars=(5,),
    )
    order, line = ring_order(fields), list(range(lax.axis_size("space")))
    ring = jnp.asarray(order, jnp.int32)[lax.axis_index("field")]
    where = jnp.stack([ring, ring % 2, lax.axis_index("space") % 2]).astype(jnp.int32)
    where = jnp.broadcast_to(where[:, None, None], (3, 8, lanes)).reshape(24, lanes)
    kinetics = jnp.pad(jnp.stack([prefactor, energy], 1), ((0, ceil - reactions), (0, 0)))
    got = lax.all_to_all(sent, "field", 0, 0, tiled=True)
    plane, edge = shape(fields, species, lanes), shape(fields // 4, species, lanes)
    x_near, x_far, flow, wiener = call(
        functools.partial(open_kernel, species),
        [plane, plane, shape(24, lanes), shape(fields, 8, lanes)],
        (got, where),
        name="open",
    )
    flops = 2 * SUB * fields * 2 * lanes * 3 * ceil * species
    cost = pl.CostEstimate(flops=8 * flops, bytes_accessed=4 << 20, transcendentals=0)

    def advance(step, pair, outs, *args):
        return call(
            functools.partial(step_kernel, step, pair),
            outs,
            (where, flow, wiener, kinetics, left, right, gain, *args),
            scratch=[
                pltpu.VMEM((2, species, fields * lanes), F32),
                pltpu.VMEM((ceil, lanes), F32),
                pltpu.VMEM((2 * ceil, species), BF16),
                pltpu.VMEM((species, ceil), BF16),
            ],
            name=f"step{step}_{pair[0]}{pair[1]}",
            cost=cost,
        )

    middle, outer = (1, 2), (0, planes - 1)
    x_halo = swaps(x_near, x_far, "space", line)
    one, two, *z_ends = advance(0, middle, [plane, plane, edge, edge], got)
    z_middle = swaps(*z_ends, "field", order)
    zero, three, *ends = advance(0, outer, [plane, plane, edge, edge, plane, plane], got, *x_halo)
    z_outer = swaps(*ends[:2], "field", order)
    x_halo = swaps(*ends[2:], "space", line)
    grid = (zero, one, two, three)
    part = advance(1, middle, shape(fields, cells // 2, lanes), *grid, *z_middle)
    done = advance(1, outer, shape(fields, cells, lanes), *grid, *z_outer, *x_halo, part)
    back = lax.all_to_all(done, "field", 0, 0, tiled=True)
    result = call(close_kernel, shape(planes, rows, species, lanes), (back,), name="close")
    return result.transpose(2, 0, 1, 3)[None]


def solution(mesh):
    return jax.shard_map(
        body,
        mesh=mesh,
        in_specs=(
            P("field", None, "space", None, None),
            P(None, "space", "field", None),
            P("space", "field", None),
            P("space", "field", None),
            P("space", "field", None),
            P(None, "field", None),
            P(),
            P(),
            P(),
            P(),
            P(),
        ),
        out_specs=P("field", None, "space", None, None),
        check_vma=False,
    )
```

```python
import functools

import jax
import jax.numpy as jnp
from jax import lax
from jax.experimental import pallas as pl
from jax.experimental.pallas import tpu as pltpu
from jax.sharding import PartitionSpec as P

STEPS = 2
SUB = 5
CHEM_STEP = 0.2
F32, BF16 = jnp.float32, jnp.bfloat16
LANES = 128
VMEM = pl.BlockSpec(memory_space=pltpu.VMEM)
SMEM = pl.BlockSpec(memory_space=pltpu.SMEM)


def lane_index(rows):
    return lax.broadcasted_iota(jnp.int32, (rows, LANES), 1)


def turn(x, shift):
    shift %= LANES
    return x if shift == 0 else pltpu.roll(x, shift, 1)


def bit(place, step):
    return (place // step) % 2 == 1


def gather_chunks(tiles, chunk):
    count = len(tiles)
    place = lane_index(tiles[0].shape[0]) // chunk
    tiles = [turn(tiles[-d], -chunk * d) for d in range(count)]
    step = 1
    while step < count:
        tiles = [jnp.where(bit(place, step), tiles[d - step], tiles[d]) for d in range(count)]
        step *= 2
    return tiles


def spread_chunks(tiles, chunk):
    count = len(tiles)
    place = lane_index(tiles[0].shape[0]) // chunk
    step = 1
    while step < count:
        tiles = [jnp.where(bit(place, step), tiles[(d + step) % count], tiles[d]) for d in range(count)]
        step *= 2
    return [turn(tiles[-y], -chunk * y) for y in range(count)]


def ring_order(count):
    half = count // 2
    return [k if k < half else half + 2 * ((count - 1 - k) // 2) + k % 2 for k in range(count)]


def pack_kernel(cur, motion, spread, mix, therm, jumps, out):
    planes, rows, species, _ = cur.shape
    parts, chunk = rows, LANES // rows
    order = ring_order(parts)
    groups = species // 8
    base = planes * species
    spot = lane_index(8) % chunk
    class_of = ((spot + 1) // 2) % 4
    for x in range(planes):
        ends = [None] * parts
        for g in range(groups):
            at = slice(8 * g, 8 * g + 8)
            tiles = gather_chunks([cur[x, y, at, :] for y in range(rows)], chunk)
            for k in range(parts):
                j = order[k]
                out[k, x * species + 8 * g : x * species + 8 * g + 8, :] = tiles[j]
                end = turn(jnp.where(spot == chunk - 1, tiles[j - 1], tiles[(j + 1) % parts]), -2 * g)
                ends[k] = end if g == 0 else jnp.where(class_of == 4 - g, end, ends[k])
        for k in range(parts):
            out[k, base + 8 + 8 * x : base + 16 + 8 * x, :] = ends[k]
    lines = [motion[c, x] for c in range(3) for x in range(planes)]
    lines += [ref[x] for ref in (spread, mix, therm) for x in range(planes)]
    blocks = [jnp.concatenate(lines[8 * a : 8 * a + 8], axis=0) for a in range(3)]
    place = lane_index(8) // chunk
    line = lax.broadcasted_iota(jnp.int32, (8, LANES), 0)
    noise = jnp.zeros((8, LANES), F32)
    for r in range(3 * STEPS):
        noise = jnp.where(line == r, jumps[r // 3, 0, r % 3], noise)
    for k in range(parts):
        j = order[k]
        packed = jnp.where(place == 3, noise, turn(blocks[0], -chunk * j))
        for a in (1, 2):
            packed = jnp.where(place == a, turn(blocks[a], chunk * (a - j)), packed)
        out[k, base : base + 8, :] = packed


def open_kernel(species, got, where, x_near, x_far, flow, wiener):
    fields = got.shape[0]
    chunk = LANES // fields
    base = 4 * species
    ring, odd = where[0:8, :], where[16:17, :] == 1
    for f in range(fields):
        first, last = got[f, 0:species, :], got[f, base - species : base, :]
        x_near[f] = jnp.where(odd, first, last)
        x_far[f] = jnp.where(odd, last, first)
    place = lane_index(8) // chunk
    for a in range(3):
        block = None
        for y in range(fields):
            piece = turn(got[y, base : base + 8, :], chunk * (y - a))
            block = piece if block is None else jnp.where(place == y, piece, block)
        step = 1
        while step < fields:
            block = jnp.where(bit(ring, step), turn(block, chunk * step), block)
            step *= 2
        flow[8 * a : 8 * a + 8, :] = block
    for f in range(fields):
        noise = got[f, base : base + 8, 3 * chunk : 3 * chunk + 1]
        wiener[f] = jnp.broadcast_to(noise, (8, LANES))


def pack_z(tile, odd, groups, skip, near, far):
    species = near.shape[1]
    spot = lane_index(species) % 8
    for g in range(groups):
        first = last = None
        for k in range(8):
            value = tile(k // 4, 4 * g + k % 4)
            lo, hi = turn(value, k), turn(value, -k)
            first = lo if k == 0 else jnp.where(spot == k, lo, first)
            last = hi if k == 0 else jnp.where(spot == 7 - k, hi, last)
        near[skip + g] = jnp.where(odd, first, last)
        far[skip + g] = jnp.where(odd, last, first)


def step_kernel(step, pair, *refs):
    where, flow, wiener, kinetics, left, right, gain, *refs = refs
    *refs, moved, arr, w, y = refs
    inner, last = pair == (1, 2), step == STEPS - 1
    fields = wiener.shape[0]
    species, reactions = gain.shape
    ceil = w.shape[0] // 2
    planes = 4
    base = planes * species
    spot = lane_index(species) % 8
    z_odd, x_odd = where[8:9, :] == 1, where[16:17, :] == 1
    if step == 0:
        got, *refs = refs

        def tile(x, f):
            return got[f, x * species : (x + 1) * species, :]

        def edges(x, f):
            rows = base + 8 + 8 * x
            packed = got[f, rows : rows + 8, :]
            value = jnp.concatenate([turn(packed, 2 * g) for g in range(4)], axis=0)
            return value, value

    else:
        *grid, z_near, z_far = refs[: planes + 2]
        refs = refs[planes + 2 :]

        def tile(x, f):
            return grid[x][f]

        def edges(x, f):
            k = 4 * pair.index(x) + f % 4
            at = (0 if inner else fields // 4) + f // 4
            near, far = z_near[at], z_far[at]
            return turn(jnp.where(z_odd, near, far), k), turn(jnp.where(z_odd, far, near), -k)

    if not inner:
        x_near, x_far, *refs = refs
        if not last:
            z_middle, refs = refs[:2], refs[2:]
    w[...] = jnp.zeros_like(w)
    for c in range(0, reactions, 16):
        end = min(c + 16, reactions)
        w[2 * c : 2 * c + end - c, :] = left[c:end, :]
        w[2 * c + 16 : 2 * c + 16 + end - c, :] = right[c:end, :]
    y[...] = jnp.zeros_like(y)
    y[:, 0:reactions] = gain[...]
    for i, x in enumerate(pair):
        row = lambda c: flow[c * planes + x : c * planes + x + 1, :]
        u = [row(0), row(1), row(2)]
        diffusion, mixing = row(3), row(4)
        total = tile(x, 0)
        for f in range(1, fields):
            total = total + tile(x, f)
        mean = (mixing * (1.0 / fields)) * total
        root = jnp.sqrt(2.0 * diffusion)
        centre = 1.0 - 6.0 * diffusion - mixing
        for f in range(fields):
            here = tile(x, f)
            sign = [0.5 * (root * wiener[f, 3 * step + d : 3 * step + d + 1, :] - u[d]) for d in range(3)]
            plus = [diffusion + s for s in sign]
            minus = [diffusion - s for s in sign]
            behind, ahead = edges(x, f)
            if x == planes - 1:
                x_plus = jnp.where(x_odd, x_far[f], x_near[f])
            else:
                x_plus = tile(x + 1, f)
            if x == 0:
                x_minus = jnp.where(x_odd, x_near[f], x_far[f])
            else:
                x_minus = tile(x - 1, f)
            value = centre * here + mean
            value = value + plus[0] * x_plus + minus[0] * x_minus
            value = value + plus[1] * turn(here, -8) + minus[1] * turn(here, 8)
            value = value + plus[2] * turn(jnp.where(spot == 0, ahead, here), -1)
            value = value + minus[2] * turn(jnp.where(spot == 7, behind, here), 1)
            moved[i, :, f * LANES : (f + 1) * LANES] = value
    pre, energy = kinetics[:, 0:1], kinetics[:, 1:2]
    count = 4
    wide = fields * LANES // count

    def chemistry(i, _):
        x = pair[0] + i * (pair[1] - pair[0])
        arr[...] = pre * jnp.exp(-energy / flow[pl.ds(5 * planes + x, 1), :])
        factor = jnp.concatenate([arr[...]] * (wide // LANES), axis=1)
        blocks = [moved[i, :, j * wide : (j + 1) * wide] for j in range(count)]

        def factors(j):
            low = blocks[j].astype(BF16)
            return [
                jnp.dot(w[2 * c : 2 * c + 32, :], low, preferred_element_type=F32)
                for c in range(0, ceil, 16)
            ]

        ahead = factors(0)
        for n in range(SUB * count):
            now, j = ahead, n % count
            if n + 1 < SUB * count:
                ahead = factors((n + 1) % count)
            rates = []
            for c, both in enumerate(now):
                f, b = both[:16], both[16:]
                scaled = factor[16 * c : 16 * c + 16] * f * b
                rates.append((scaled / (1.0 + f * f + b * b)).astype(BF16))
            rates = jnp.concatenate(rates, axis=0)
            blocks[j] = blocks[j] + CHEM_STEP * jnp.dot(y[...], rates, preferred_element_type=F32)
        for j in range(count):
            moved[i, :, j * wide : (j + 1) * wide] = blocks[j]
        return 0

    lax.fori_loop(0, 2, chemistry, 0)
    result = lambda i, f: moved[i, :, f * LANES : (f + 1) * LANES]
    if not last:
        for i in range(2):
            for f in range(fields):
                refs[i][f] = result(i, f)
        pack_z(result, z_odd, fields // 4, 0 if inner else fields // 4, *refs[2:4])
        if not inner:
            for g in range(fields // 4):
                refs[2][g] = z_middle[0][g]
                refs[3][g] = z_middle[1][g]
            for f in range(fields):
                refs[4][f] = jnp.where(x_odd, result(0, f), result(1, f))
                refs[5][f] = jnp.where(x_odd, result(1, f), result(0, f))
    elif inner:
        for i in range(2):
            for f in range(fields):
                refs[0][f, i * species : (i + 1) * species, :] = result(i, f)
    else:
        middle, out = refs
        for f in range(fields):
            out[f, 0:species, :] = result(0, f)
            out[f, species : base - species, :] = middle[f]
            out[f, base - species : base, :] = result(1, f)


def close_kernel(got, out):
    planes, rows, species, _ = out.shape
    chunk = LANES // rows
    order = ring_order(rows)
    for x in range(planes):
        for g in range(species // 8):
            at = x * species + 8 * g
            tiles = [got[order.index(j), at : at + 8, :] for j in range(rows)]
            tiles = spread_chunks(tiles, chunk)
            for y in range(rows):
                out[x, y, 8 * g : 8 * g + 8, :] = tiles[y]


def shape(*dims):
    return jax.ShapeDtypeStruct(dims, F32)


def call(kernel, outs, args, scratch=(), name=None, cost=None, scalars=()):
    many = isinstance(outs, (list, tuple))
    return pl.pallas_call(
        kernel,
        out_shape=outs,
        in_specs=[SMEM if i in scalars else VMEM for i in range(len(args))],
        out_specs=[VMEM] * len(outs) if many else VMEM,
        scratch_shapes=list(scratch),
        name=name,
        cost_estimate=cost,
        compiler_params=pltpu.CompilerParams(vmem_limit_bytes=40 << 20),
    )(*args)


def swaps(near, far, axis, order):
    count = len(order)
    pairs = lambda first: [
        (order.index((q + first) % count), order.index((p + first) % count))
        for i in range(0, count, 2)
        for p, q in ((i, i + 1), (i + 1, i))
    ]
    return lax.ppermute(near, axis, pairs(0)), lax.ppermute(far, axis, pairs(1))


def body(comp, motion, spread, mix, therm, jumps, left, right, gain, prefactor, energy):
    fields = lax.axis_size("field")
    _, species, planes, rows, lanes = comp.shape
    reactions = left.shape[0]
    ceil = -(-reactions // 16) * 16
    cells = planes * species
    turned = comp[0].transpose(1, 2, 0, 3)
    sent = call(
        pack_kernel,
        shape(fields, cells + 40, lanes),
        (turned, motion, spread, mix, therm, jumps),
        name="pack",
        scalars=(5,),
    )
    order, line = ring_order(fields), list(range(lax.axis_size("space")))
    ring = jnp.asarray(order, jnp.int32)[lax.axis_index("field")]
    where = jnp.stack([ring, ring % 2, lax.axis_index("space") % 2]).astype(jnp.int32)
    where = jnp.broadcast_to(where[:, None, None], (3, 8, lanes)).reshape(24, lanes)
    kinetics = jnp.pad(jnp.stack([prefactor, energy], 1), ((0, ceil - reactions), (0, 0)))
    got = lax.all_to_all(sent, "field", 0, 0, tiled=True)
    plane, edge = shape(fields, species, lanes), shape(fields // 4, species, lanes)
    x_near, x_far, flow, wiener = call(
        functools.partial(open_kernel, species),
        [plane, plane, shape(24, lanes), shape(fields, 8, lanes)],
        (got, where),
        name="open",
    )
    flops = 2 * SUB * fields * 2 * lanes * 3 * ceil * species
    cost = pl.CostEstimate(flops=8 * flops, bytes_accessed=4 << 20, transcendentals=0)

    def advance(step, pair, outs, *args):
        return call(
            functools.partial(step_kernel, step, pair),
            outs,
            (where, flow, wiener, kinetics, left, right, gain, *args),
            scratch=[
                pltpu.VMEM((2, species, fields * lanes), F32),
                pltpu.VMEM((ceil, lanes), F32),
                pltpu.VMEM((2 * ceil, species), BF16),
                pltpu.VMEM((species, ceil), BF16),
            ],
            name=f"step{step}_{pair[0]}{pair[1]}",
            cost=cost,
        )

    middle, outer = (1, 2), (0, planes - 1)
    x_halo = swaps(x_near, x_far, "space", line)
    one, two, *z_ends = advance(0, middle, [plane, plane, edge, edge], got)
    edge = shape(fields // 2, species, lanes)
    zero, three, *ends = advance(0, outer, [plane, plane, edge, edge, plane, plane], got, *x_halo, *z_ends)
    z_halo = swaps(*ends[:2], "field", order)
    x_halo = swaps(*ends[2:], "space", line)
    grid = (zero, one, two, three)
    part = advance(1, middle, shape(fields, cells // 2, lanes), *grid, *z_halo)
    done = advance(1, outer, shape(fields, cells, lanes), *grid, *z_halo, *x_halo, part)
    back = lax.all_to_all(done, "field", 0, 0, tiled=True)
    result = call(close_kernel, shape(planes, rows, species, lanes), (back,), name="close")
    return result.transpose(2, 0, 1, 3)[None]


def solution(mesh):
    return jax.shard_map(
        body,
        mesh=mesh,
        in_specs=(
            P("field", None, "space", None, None),
            P(None, "space", "field", None),
            P("space", "field", None),
            P("space", "field", None),
            P("space", "field", None),
            P(None, "field", None),
            P(),
            P(),
            P(),
            P(),
            P(),
        ),
        out_specs=P("field", None, "space", None, None),
        check_vma=False,
    )
```
